32 devices in a mesh: groups: 2 (over y), chan: 8 (over z, x), pair: 2 (over core).
Axes of the slice: x: 2, y: 2, z: 4, core: 2. Of those that a mesh axis runs over, the one named last changes fastest.
Arguments:
- raw: bfloat16 [1024, 1, 12000], P(('groups', 'chan')), parts along dimension 0, may hold values from -6 to 6
- live_index: int32 [16, 64], P(('groups', 'chan')), parts along dimension 0, may hold values from 0 to 63, each once within a row
- live_count: int32 [16], P('groups'), parts along dimension 0, may hold values from 1 to 64, 256 in all
Outputs:
- correlation: bfloat16 [6, 1024, 512], P('pair', ('groups', 'chan')), parts along dimension 1
The draws below stay inside these ranges and needn't reach their ends.
There are 2 independent parts, one for each index of `groups`. The reference program is written for one: setup_inputs(seed, part) draws one part's arguments, and reference() takes and returns one part's arrays. A program takes and returns all parts, laid end to end along the dimension named above; each array names one. Nothing has to cross between parts.
Inputs may be any that keep to these rules, and one draw needn't show every extreme that they name: `live_index`: each block's row is a permutation of the raw channels of that block. `live_count`: live slots of each block; they sum to 256, and some block fills all 64 slots.
All inputs are finite; a program needn't handle non-finite values.
Results may differ from the reference program's by a relative error of at most 0.001.
The reference program's roundings to bfloat16 on the way (of `picked`, `dft_table`, `whitened` and `weighted`) count: a program that leaves them out, or rounds other values in their place, can miss the bound.
Values may be sent and summed in bfloat16 or wider, within the bound.
A program may use at most 128 MiB of HBM per device.

```python
import math
import jax
import jax.numpy as jnp
import numpy as np
from jax import lax

S = 12000
NB = 448
NSEG = 1
L = 6
LSTEP = 125
F0 = 60
CAP = 64
BLOCKS = 8
SLOTS = 512
LIVE = 256


def level_of(own_key, extent, pieces, least, high):
    gain = 1.0
    for position, shards_of in pieces:
        steps = jax.random.uniform(jax.random.fold_in(jax.random.fold_in(own_key, 6), position), (shards_of,), jnp.float32, least / len(pieces), high / len(pieces))
        gain = gain * jnp.repeat(jnp.exp(steps), extent[position] // shards_of).reshape((-1,) + (1,) * (len(extent) - 1 - position))
    return gain


def split_up(amount, total, most, lean):
    loads = [(1 << 20) // math.isqrt(grade ** lean) + 1 for grade in range(2, amount + 1)]
    spare, holding = total - most - (amount - 1), [1] * (amount - 1)
    while spare > 0:
        candidates = [i for i in range(amount - 1) if holding[i] < most]
        whole, budget = sum([loads[i] for i in candidates]), spare
        for i in candidates:
            extra = min(most - holding[i], max(1, budget * loads[i] // whole), spare)
            holding[i] = holding[i] + extra
            spare = spare - extra
    return np.array([most] + holding)


def uneven_parts(rng, count, total, bound, lean):
    if count == 2:
        one = jax.random.randint(rng, (), max(1, total - bound), min(bound, total - 1) + 1)
        return jnp.stack([one, total - one])
    lengths = jnp.asarray(split_up(count, total, bound, lean), jnp.int32)
    twos = (count - 1) // 2
    source_of, receiver = lengths[1:1 + 2 * twos:2], lengths[2:2 + 2 * twos:2]
    slack = jnp.minimum(source_of - 1, bound - receiver)
    passed = jax.random.randint(jax.random.fold_in(rng, 1), (twos,), 0, 1 << 20) % (slack + 1)
    lengths = lengths.at[1:1 + 2 * twos:2].set(source_of - passed).at[2:2 + 2 * twos:2].set(receiver + passed)
    return lengths[jax.random.permutation(jax.random.fold_in(rng, 2), count)]


def gaussian(key, shape, spread, reach, pieces=(), held_as=jnp.bfloat16):
    drawn = jax.random.normal(key, shape, jnp.float32) * spread
    if len(pieces) > 0:
        drawn = level_of(key, shape, pieces, -0.22, 0.18) * drawn
    return jnp.clip(drawn, min=-reach, max=reach).astype(held_as)


def setup_inputs(seed: int = 0, part: int = 0) -> dict:
    key_list = jax.random.split(jax.random.key(seed), 4)
    part_splits = jax.random.split(jax.random.fold_in(key_list[3], part), 4)
    raw = gaussian(part_splits[0], (SLOTS, NSEG, S), 1.0, 6.0, ((0, 8),))
    live_index = jax.vmap(lambda own: jax.random.permutation(own, CAP))(jax.random.split(part_splits[1], BLOCKS)).reshape((BLOCKS, CAP)).astype(jnp.int32)
    live_count = uneven_parts(part_splits[2], BLOCKS, LIVE, CAP, 2).astype(jnp.int32)
    return dict(raw=raw, live_index=live_index, live_count=live_count)


water_level = 0.1

def lag_weights(lag_ids, bin_ids):
    band_taper = 0.5 - 0.5 * jnp.cos(2.0 * jnp.pi * (bin_ids.astype(jnp.float32) + 0.5) / NB)
    phase_int = (F0 + bin_ids)[None, :] * lag_ids[:, None] % S
    waves = jnp.cos(phase_int.astype(jnp.float32) * (2.0 * jnp.pi / S))
    return band_taper[None, :] * waves / jnp.sqrt(jnp.float32(NSEG * NB))

def reference(raw, live_index, live_count):
    blocks = live_count.shape[0]
    raw_rows = (jnp.arange(blocks, dtype=jnp.int32)[:, None] * CAP + live_index).reshape(-1).astype(jnp.int32)
    live_mask = (jnp.arange(CAP, dtype=jnp.int32)[None, :] < live_count[:, None]).reshape(-1)
    picked = jnp.where(live_mask[:, None, None], raw[raw_rows], jnp.zeros((), raw.dtype))
    sample_ids = jnp.arange(S, dtype=jnp.int32)
    bin_ids = jnp.arange(NB, dtype=jnp.int32)
    phase_int = sample_ids[:, None] * (F0 + bin_ids)[None, :] % S
    angles = phase_int.astype(jnp.float32) * (2.0 * jnp.pi / S)
    dft_table = jnp.concatenate([jnp.cos(angles), -jnp.sin(angles)], axis=1).astype(jnp.bfloat16)
    spectrum = jnp.dot(picked.reshape(-1, S), dft_table, preferred_element_type=jnp.float32)
    spectrum = spectrum.reshape(SLOTS, NSEG, 2, NB)
    band_power = lax.optimization_barrier(jnp.sum(spectrum * spectrum, axis=(2, 3))) / NB
    magnitude = spectrum[:, :, 0] ** 2 + spectrum[:, :, 1] ** 2
    denom = jnp.sqrt(magnitude + water_level * band_power[:, :, None] + 1e-06)
    whitened = (spectrum / denom[:, :, None, :]).astype(jnp.bfloat16)
    flat_spectra = whitened.reshape(SLOTS, -1)
    lag_ids = (jnp.arange(L, dtype=jnp.int32) * LSTEP).astype(jnp.int32)
    weights = lag_weights(lag_ids, bin_ids)

    def per_lag(weight_row):
        weighted = (whitened.astype(jnp.float32) * weight_row[None, None, None, :]).astype(jnp.bfloat16)
        product = lax.dot_general(weighted.reshape(SLOTS, -1), flat_spectra, (((1,), (1,)), ((), ())), preferred_element_type=jnp.float32)
        return product.astype(jnp.bfloat16)
    return lax.map(per_lag, weights)
```

```python
import functools

import jax
import jax.numpy as jnp
import numpy as np
from jax import lax
from jax.experimental import pallas as pl
from jax.experimental.pallas import tpu as pltpu
from jax.sharding import PartitionSpec as P

S = 12000
NB = 448
L = 6
LSTEP = 125
F0 = 60
WATER = 0.1
QUARTER = S // 4
CHUNK = 256
NCHUNK = -(-QUARTER // CHUNK)
PADB = 512
COLS = 2 * NB


def phase_rows(steps):
    k = F0 + np.arange(NB)
    angle = 2.0 * np.pi * ((np.asarray(steps)[:, None] * k[None, :]) % S) / S
    out = np.zeros((len(steps), 2 * PADB), np.float32)
    out[:, :NB] = np.cos(angle)
    out[:, PADB : PADB + NB] = -np.sin(angle)
    return out


def twiddles():
    fine = phase_rows(np.arange(16))
    mid = phase_rows(16 * np.arange(16))
    return np.concatenate([fine, mid], axis=0)


def coarse_twiddles():
    coarse = phase_rows(CHUNK * np.arange(NCHUNK))
    return np.repeat(coarse[:, None, :], 8, axis=1)


def column_bins():
    tail = np.arange(384, NB)
    return np.concatenate([np.arange(384), np.arange(384), tail, tail])


def lag_table():
    j = column_bins()
    taper = 0.5 - 0.5 * np.cos(2.0 * np.pi * (j + 0.5) / NB)
    lags = np.arange(L)[:, None] * LSTEP
    waves = np.cos(2.0 * np.pi * (((F0 + j)[None, :] * lags) % S) / S)
    table = np.zeros((2, 8, COLS), np.float32)
    table[:, : L // 2] = (taper[None, :] * waves / np.sqrt(NB)).reshape(2, L // 2, COLS)
    return table


def make_table(tw_ref, coarse_ref, base_ref, table_ref):
    for a in range(16):
        for v in range(PADB // 128):
            c_cols = slice(128 * v, 128 * v + 128)
            s_cols = slice(PADB + 128 * v, PADB + 128 * v + 128)
            fc, fs = tw_ref[0:16, c_cols], tw_ref[0:16, s_cols]
            mc, ms = tw_ref[16 + a : 17 + a, c_cols], tw_ref[16 + a : 17 + a, s_cols]
            base_ref[16 * a : 16 * a + 16, c_cols] = fc * mc - fs * ms
            base_ref[16 * a : 16 * a + 16, s_cols] = fs * mc + fc * ms

    def chunk(i, carry):
        row0 = pl.multiple_of(i * CHUNK, CHUNK)
        for v in range(PADB // 128):
            c_cols = slice(128 * v, 128 * v + 128)
            s_cols = slice(PADB + 128 * v, PADB + 128 * v + 128)
            cc = coarse_ref[i, 0:1, c_cols]
            cs = coarse_ref[i, 0:1, s_cols]
            for r in range(0, CHUNK, 16):
                bc, bs = base_ref[r : r + 16, c_cols], base_ref[r : r + 16, s_cols]
                rows = pl.ds(row0 + r, 16)
                table_ref[rows, c_cols] = (bc * cc - bs * cs).astype(jnp.bfloat16)
                table_ref[rows, s_cols] = (bs * cc + bc * cs).astype(jnp.bfloat16)
        return carry

    lax.fori_loop(0, NCHUNK, chunk, 0)


def whiten_rows(spec_ref, slots):
    def quarter(q, part):
        return spec_ref[slots * q : slots * (q + 1), PADB * part : PADB * (part + 1)]

    a0, a1, a2, a3 = (quarter(q, 0) for q in range(4))
    b0, b1, b2, b3 = (quarter(q, 1) for q in range(4))
    m = lax.broadcasted_iota(jnp.int32, (slots, PADB), 1) % 4
    even = m % 2 == 0
    sign = jnp.where(m < 2, 1.0, -1.0)
    re = jnp.where(even, a0 + a2 + sign * (a1 + a3), a0 - a2 + sign * (b1 - b3))
    im = jnp.where(even, b0 + b2 + sign * (b1 + b3), b0 - b2 - sign * (a1 - a3))
    mag = re * re + im * im
    power = jnp.sum(mag, axis=1, keepdims=True) / NB
    denom = jnp.sqrt(mag + WATER * power + 1e-06)
    re, im = re / denom, im / denom
    tail = re[:, 384:] + pltpu.roll(im[:, 384:], 64, 1)
    return jnp.concatenate([re[:, :384], im[:, :384], tail], axis=1).astype(jnp.bfloat16)


def kernel(
    n,
    raw_hbm,
    index_ref,
    count_ref,
    tw_ref,
    coarse_ref,
    lagw_ref,
    out_ref,
    x_ref,
    xq_ref,
    base_ref,
    table_ref,
    spec_ref,
    spread_ref,
    lagged_ref,
    load_sem,
    send_sem,
    recv_sem,
    fsend_sem,
    frecv_sem,
):
    slots = raw_hbm.shape[0]
    half = slots // 2
    me = lax.axis_index("chan")
    core = lax.axis_index("pair")
    other = 1 - core

    load = pltpu.make_async_copy(raw_hbm, x_ref, load_sem)
    load.start()

    barrier = pltpu.get_barrier_semaphore()
    pl.semaphore_signal(barrier, inc=1, device_id={"pair": other})
    for d in range(1, n):
        pl.semaphore_signal(barrier, inc=1, device_id={"chan": lax.rem(me + d, n)})

    make_table(tw_ref, coarse_ref, base_ref, table_ref)
    load.wait()
    for q in range(4):
        rows = slice(slots * q, slots * (q + 1))
        xq_ref[rows, 0:QUARTER] = x_ref[:, QUARTER * q : QUARTER * (q + 1)]
        pad = NCHUNK * CHUNK - QUARTER
        xq_ref[rows, QUARTER:] = jnp.zeros((slots, pad), jnp.bfloat16)
    for v in range(2 * PADB // 256):
        cols = slice(256 * v, 256 * v + 256)
        spec_ref[:, cols] = jnp.dot(
            xq_ref[...], table_ref[:, cols], preferred_element_type=jnp.float32
        )
    whitened = whiten_rows(spec_ref, slots)

    r_ids = lax.broadcasted_iota(jnp.int32, (slots, slots), 0)
    k_ids = lax.broadcasted_iota(jnp.int32, (slots, slots), 1)
    chosen = (index_ref[...] == r_ids) & (k_ids < count_ref[me])
    pick = jnp.where(chosen, 1.0, 0.0).T.astype(jnp.bfloat16)
    own = jnp.dot(pick, whitened, preferred_element_type=jnp.float32)
    own16 = own.astype(jnp.bfloat16)
    spread_ref[pl.ds(pl.multiple_of(me * slots, slots), slots), :] = own16

    def part(block, who):
        return spread_ref.at[pl.ds(pl.multiple_of(block * slots + who * half, half), half), :]

    pl.semaphore_wait(barrier, n)

    def direct(d):
        return pltpu.make_async_remote_copy(
            src_ref=part(me, core),
            dst_ref=part(me, core),
            send_sem=send_sem.at[d],
            recv_sem=recv_sem.at[d],
            device_id={"chan": lax.rem(me + d, n)},
        )

    def arrival(d):
        block = lax.rem(me - d + n, n)
        return pltpu.make_async_remote_copy(
            src_ref=part(block, core),
            dst_ref=part(block, core),
            send_sem=send_sem.at[d],
            recv_sem=recv_sem.at[d],
            device_id={"chan": lax.rem(me + d, n)},
        )

    def forward(d, who):
        block = lax.rem(me - d + n, n)
        return pltpu.make_async_remote_copy(
            src_ref=part(block, who),
            dst_ref=part(block, who),
            send_sem=fsend_sem.at[d],
            recv_sem=frecv_sem.at[d],
            device_id={"pair": other},
        )

    for d in range(1, n):
        direct(d).start()
    for l in range(L // 2):
        weight = lagw_ref[core, l : l + 1, :]
        lagged_ref[slots * l : slots * (l + 1), :] = (own * weight).astype(jnp.bfloat16)
    for d in range(1, n):
        arrival(d).wait_recv()
        forward(d, core).start()
    for d in range(1, n):
        forward(d, other).wait_recv()
    for d in range(1, n):
        direct(d).wait_send()
        forward(d, core).wait_send()

    def columns(g, carry):
        at = pl.multiple_of(g * 512, 512)
        product = lax.dot_general(
            lagged_ref[...],
            spread_ref[pl.ds(at, 512), :],
            (((1,), (1,)), ((), ())),
            preferred_element_type=jnp.float32,
        ).astype(jnp.bfloat16)
        for l in range(L // 2):
            out_ref[l, :, pl.ds(at, 512)] = product[slots * l : slots * (l + 1)]
        return carry

    lax.fori_loop(0, n * slots // 512, columns, 0)


def shards(n, raw, live_index, live_count):
    slots = raw.shape[0]
    vmem = pl.BlockSpec(memory_space=pltpu.VMEM)
    return pl.pallas_call(
        functools.partial(kernel, n),
        out_shape=jax.ShapeDtypeStruct((L // 2, slots, n * slots), jnp.bfloat16),
        in_specs=[
            pl.BlockSpec(memory_space=pl.ANY),
            vmem,
            pl.BlockSpec(memory_space=pltpu.SMEM),
            vmem,
            vmem,
            vmem,
        ],
        out_specs=vmem,
        scratch_shapes=[
            pltpu.VMEM((slots, S), jnp.bfloat16),
            pltpu.VMEM((4 * slots, NCHUNK * CHUNK), jnp.bfloat16),
            pltpu.VMEM((CHUNK, 2 * PADB), jnp.float32),
            pltpu.VMEM((NCHUNK * CHUNK, 2 * PADB), jnp.bfloat16),
            pltpu.VMEM((4 * slots, 2 * PADB), jnp.float32),
            pltpu.VMEM((n * slots, COLS), jnp.bfloat16),
            pltpu.VMEM((L // 2 * slots, COLS), jnp.bfloat16),
            pltpu.SemaphoreType.DMA,
            pltpu.SemaphoreType.DMA((n,)),
            pltpu.SemaphoreType.DMA((n,)),
            pltpu.SemaphoreType.DMA((n,)),
            pltpu.SemaphoreType.DMA((n,)),
        ],
        compiler_params=pltpu.CompilerParams(
            collective_id=0, has_side_effects=True, vmem_limit_bytes=60 * 1024 * 1024
        ),
    )(
        raw.reshape(slots, S),
        live_index,
        live_count,
        jnp.asarray(twiddles()),
        jnp.asarray(coarse_twiddles()),
        jnp.asarray(lag_table()),
    )


def solution(mesh):
    return jax.shard_map(
        functools.partial(shards, mesh.shape["chan"]),
        mesh=mesh,
        in_specs=(P(("groups", "chan"), None, None), P(("groups", "chan"), None), P("groups")),
        out_specs=P("pair", ("groups", "chan"), None),
        check_vma=False,
    )
```

```python
import functools

import jax
import jax.numpy as jnp
import numpy as np
from jax import lax
from jax.experimental import pallas as pl
from jax.experimental.pallas import tpu as pltpu
from jax.sharding import PartitionSpec as P

S = 12000
NB = 448
L = 6
LSTEP = 125
F0 = 60
WATER = 0.1
QUARTER = S // 4
CHUNK = 256
NCHUNK = -(-QUARTER // CHUNK)
PADB = 512
COLS = 2 * NB


def phase_rows(steps, shift=0.0):
    k = F0 + np.arange(NB)
    angle = 2.0 * np.pi * ((np.asarray(steps)[:, None] * k[None, :]) % S) / S + shift
    out = np.zeros((len(steps), 2 * PADB), np.float32)
    out[:, :NB] = np.cos(angle)
    out[:, PADB : PADB + NB] = -np.sin(angle)
    return out


def twiddles():
    step = 2.0 * np.pi / S
    fine = phase_rows(np.arange(16), np.pi * (float(np.float32(step)) / step - 1.0))
    mid = phase_rows(16 * np.arange(16))
    return np.concatenate([fine, mid], axis=0)


def coarse_twiddles():
    coarse = phase_rows(CHUNK * np.arange(NCHUNK))
    return np.repeat(coarse[:, None, :], 8, axis=1)


def column_bins():
    tail = np.arange(384, NB)
    return np.concatenate([np.arange(384), np.arange(384), tail, tail])


def lag_table():
    j = column_bins()
    taper = 0.5 - 0.5 * np.cos(2.0 * np.pi * (j + 0.5) / NB)
    lags = np.arange(L)[:, None] * LSTEP
    waves = np.cos(2.0 * np.pi * (((F0 + j)[None, :] * lags) % S) / S)
    table = np.zeros((2, 8, COLS), np.float32)
    table[:, : L // 2] = (taper[None, :] * waves / np.sqrt(NB)).reshape(2, L // 2, COLS)
    return table


def make_table(tw_ref, coarse_ref, base_ref, table_ref):
    for a in range(16):
        for v in range(PADB // 128):
            c_cols = slice(128 * v, 128 * v + 128)
            s_cols = slice(PADB + 128 * v, PADB + 128 * v + 128)
            fc, fs = tw_ref[0:16, c_cols], tw_ref[0:16, s_cols]
            mc, ms = tw_ref[16 + a : 17 + a, c_cols], tw_ref[16 + a : 17 + a, s_cols]
            base_ref[16 * a : 16 * a + 16, c_cols] = fc * mc - fs * ms
            base_ref[16 * a : 16 * a + 16, s_cols] = fs * mc + fc * ms

    def chunk(i, carry):
        row0 = pl.multiple_of(i * CHUNK, CHUNK)
        for v in range(PADB // 128):
            c_cols = slice(128 * v, 128 * v + 128)
            s_cols = slice(PADB + 128 * v, PADB + 128 * v + 128)
            cc = coarse_ref[i, 0:1, c_cols]
            cs = coarse_ref[i, 0:1, s_cols]
            for r in range(0, CHUNK, 16):
                bc, bs = base_ref[r : r + 16, c_cols], base_ref[r : r + 16, s_cols]
                rows = pl.ds(row0 + r, 16)
                table_ref[rows, c_cols] = (bc * cc - bs * cs).astype(jnp.bfloat16)
                table_ref[rows, s_cols] = (bs * cc + bc * cs).astype(jnp.bfloat16)
        return carry

    lax.fori_loop(0, NCHUNK, chunk, 0)


def whiten_rows(spec_ref, slots):
    def quarter(q, part):
        return spec_ref[slots * q : slots * (q + 1), PADB * part : PADB * (part + 1)]

    a0, a1, a2, a3 = (quarter(q, 0) for q in range(4))
    b0, b1, b2, b3 = (quarter(q, 1) for q in range(4))
    m = lax.broadcasted_iota(jnp.int32, (slots, PADB), 1) % 4
    even = m % 2 == 0
    sign = jnp.where(m < 2, 1.0, -1.0)
    re = jnp.where(even, a0 + a2 + sign * (a1 + a3), a0 - a2 + sign * (b1 - b3))
    im = jnp.where(even, b0 + b2 + sign * (b1 + b3), b0 - b2 - sign * (a1 - a3))
    mag = re * re + im * im
    power = jnp.sum(mag, axis=1, keepdims=True) / NB
    denom = jnp.sqrt(mag + WATER * power + 1e-06)
    re, im = re / denom, im / denom
    tail = re[:, 384:] + pltpu.roll(im[:, 384:], 64, 1)
    return jnp.concatenate([re[:, :384], im[:, :384], tail], axis=1).astype(jnp.bfloat16)


def kernel(
    n,
    raw_hbm,
    index_ref,
    count_ref,
    tw_ref,
    coarse_ref,
    lagw_ref,
    out_ref,
    x_ref,
    xq_ref,
    base_ref,
    table_ref,
    spec_ref,
    spread_ref,
    lagged_ref,
    load_sem,
    zsend_sem,
    zrecv_sem,
    xsend_sem,
    xrecv_sem,
    fsend_sem,
    frecv_sem,
):
    slots = raw_hbm.shape[0]
    half = slots // 2
    me = lax.axis_index("chan")
    core = lax.axis_index("pair")
    other = 1 - core

    load = pltpu.make_async_copy(raw_hbm, x_ref, load_sem)
    load.start()

    lines = n // 2
    line, side = me // 2, lax.rem(me, 2)
    mate = 2 * line + 1 - side
    order = sorted(range(1, lines), key=lambda d: min(d, lines - d))

    def chip(d, which):
        return 2 * lax.rem(line + d + lines, lines) + which

    barrier = pltpu.get_barrier_semaphore()
    pl.semaphore_signal(barrier, inc=1, device_id={"pair": other})
    pl.semaphore_signal(barrier, inc=1, device_id={"chan": mate})
    for d in order:
        pl.semaphore_signal(barrier, inc=1, device_id={"chan": chip(d, side)})

    make_table(tw_ref, coarse_ref, base_ref, table_ref)
    load.wait()
    for q in range(4):
        rows = slice(slots * q, slots * (q + 1))
        xq_ref[rows, 0:QUARTER] = x_ref[:, QUARTER * q : QUARTER * (q + 1)]
        pad = NCHUNK * CHUNK - QUARTER
        xq_ref[rows, QUARTER:] = jnp.zeros((slots, pad), jnp.bfloat16)
    for v in range(2 * PADB // 256):
        cols = slice(256 * v, 256 * v + 256)
        spec_ref[:, cols] = jnp.dot(
            xq_ref[...], table_ref[:, cols], preferred_element_type=jnp.float32
        )
    whitened = whiten_rows(spec_ref, slots)

    r_ids = lax.broadcasted_iota(jnp.int32, (slots, slots), 0)
    k_ids = lax.broadcasted_iota(jnp.int32, (slots, slots), 1)
    chosen = (index_ref[...] == r_ids) & (k_ids < count_ref[me])
    pick = jnp.where(chosen, 1.0, 0.0).T.astype(jnp.bfloat16)
    own = jnp.dot(pick, whitened, preferred_element_type=jnp.float32)
    own16 = own.astype(jnp.bfloat16)
    spread_ref[pl.ds(pl.multiple_of(me * slots, slots), slots), :] = own16

    def part(block, who):
        return spread_ref.at[pl.ds(pl.multiple_of(block * slots + who * half, half), half), :]

    pl.semaphore_wait(barrier, lines + 1)

    def copy(block, who, sends, recvs, at, device_id):
        ref = part(block, who)
        return pltpu.make_async_remote_copy(
            src_ref=ref,
            dst_ref=ref,
            send_sem=sends.at[at],
            recv_sem=recvs.at[at],
            device_id=device_id,
        )

    def along(d, block):
        return copy(block, core, zsend_sem, zrecv_sem, d, {"chan": chip(d, side)})

    def across(d, which):
        return copy(chip(-d, which), core, xsend_sem, xrecv_sem, d, {"chan": mate})

    def inside(d, which, who):
        at = d + lines * (1 if which is side else 0)
        return copy(chip(-d, which), who, fsend_sem, frecv_sem, at, {"pair": other})

    far = 1 - side
    across(0, side).start()
    for d in order:
        along(d, me).start()
    for l in range(L // 2):
        weight = lagw_ref[core, l : l + 1, :]
        lagged_ref[slots * l : slots * (l + 1), :] = (own * weight).astype(jnp.bfloat16)

    across(0, far).wait_recv()
    inside(0, far, core).start()
    for d in order:
        along(d, chip(-d, side)).wait_recv()
        across(d, side).start()
        inside(d, side, core).start()

    for i, d in enumerate([0] + order):
        if d > 0:
            across(d, far).wait_recv()
            inside(d, far, core).start()
            inside(d, side, other).wait_recv()
        inside(d, far, other).wait_recv()
        at = pl.multiple_of(chip(-d, 0) * slots, 2 * slots)
        product = lax.dot_general(
            lagged_ref[...],
            spread_ref[pl.ds(at, 2 * slots), :],
            (((1,), (1,)), ((), ())),
            preferred_element_type=jnp.float32,
        ).astype(jnp.bfloat16)
        for l in range(L // 2):
            out_ref[l, :, pl.ds(at, 2 * slots)] = product[slots * l : slots * (l + 1)]

    for d in [0] + order:
        across(d, side).wait_send()
        inside(d, far, core).wait_send()
        if d > 0:
            along(d, me).wait_send()
            inside(d, side, core).wait_send()


def shards(n, raw, live_index, live_count):
    slots = raw.shape[0]
    vmem = pl.BlockSpec(memory_space=pltpu.VMEM)
    return pl.pallas_call(
        functools.partial(kernel, n),
        out_shape=pltpu.VMEM((L // 2, slots, n * slots), jnp.bfloat16),
        in_specs=[
            pl.BlockSpec(memory_space=pl.ANY),
            vmem,
            pl.BlockSpec(memory_space=pltpu.SMEM),
            vmem,
            vmem,
            vmem,
        ],
        out_specs=vmem,
        scratch_shapes=[
            pltpu.VMEM((slots, S), jnp.bfloat16),
            pltpu.VMEM((4 * slots, NCHUNK * CHUNK), jnp.bfloat16),
            pltpu.VMEM((CHUNK, 2 * PADB), jnp.float32),
            pltpu.VMEM((NCHUNK * CHUNK, 2 * PADB), jnp.bfloat16),
            pltpu.VMEM((4 * slots, 2 * PADB), jnp.float32),
            pltpu.VMEM((n * slots, COLS), jnp.bfloat16),
            pltpu.VMEM((L // 2 * slots, COLS), jnp.bfloat16),
            pltpu.SemaphoreType.DMA,
            pltpu.SemaphoreType.DMA((n // 2,)),
            pltpu.SemaphoreType.DMA((n // 2,)),
            pltpu.SemaphoreType.DMA((n // 2,)),
            pltpu.SemaphoreType.DMA((n // 2,)),
            pltpu.SemaphoreType.DMA((n,)),
            pltpu.SemaphoreType.DMA((n,)),
        ],
        compiler_params=pltpu.CompilerParams(
            collective_id=0, has_side_effects=True, vmem_limit_bytes=44 * 1024 * 1024
        ),
    )(
        raw.reshape(slots, S),
        live_index,
        live_count,
        jnp.asarray(twiddles()),
        jnp.asarray(coarse_twiddles()),
        jnp.asarray(lag_table()),
    )


def solution(mesh):
    return jax.shard_map(
        functools.partial(shards, mesh.shape["chan"]),
        mesh=mesh,
        in_specs=(P(("groups", "chan"), None, None), P(("groups", "chan"), None), P("groups")),
        out_specs=P("pair", ("groups", "chan"), None),
        check_vma=False,
    )
```

```python
import functools

import jax
import jax.numpy as jnp
import numpy as np
from jax import lax
from jax.experimental import pallas as pl
from jax.experimental.pallas import tpu as pltpu
from jax.sharding import PartitionSpec as P

S = 12000
NB = 448
L = 6
LSTEP = 125
F0 = 60
WATER = 0.1
QUARTER = S // 4
CHUNK = 256
NCHUNK = -(-QUARTER // CHUNK)
PADB = 512
COLS = 2 * NB
VMEM_LIMIT = 63_300_000


def phase_rows(steps, shift=0.0):
    k = F0 + np.arange(NB)
    angle = 2.0 * np.pi * ((np.asarray(steps)[:, None] * k[None, :]) % S) / S + shift
    out = np.zeros((len(steps), 2 * PADB), np.float32)
    out[:, :NB] = np.cos(angle)
    out[:, PADB : PADB + NB] = -np.sin(angle)
    return out


def constants():
    step = 2.0 * np.pi / S
    fine = phase_rows(np.arange(16), np.pi * (float(np.float32(step)) / step - 1.0))
    mid = phase_rows(16 * np.arange(16))
    coarse = np.repeat(phase_rows(CHUNK * np.arange(NCHUNK)), 8, axis=0)
    return np.concatenate([fine, mid, coarse, lag_table()], axis=0)


def column_bins():
    tail = np.arange(384, NB)
    return np.concatenate([np.arange(384), np.arange(384), tail, tail])


def lag_table():
    j = column_bins()
    taper = 0.5 - 0.5 * np.cos(2.0 * np.pi * (j + 0.5) / NB)
    lags = np.arange(L)[:, None] * LSTEP
    waves = np.cos(2.0 * np.pi * (((F0 + j)[None, :] * lags) % S) / S)
    table = np.zeros((2, 8, 2 * PADB), np.float32)
    table[:, : L // 2, :COLS] = (taper[None, :] * waves / np.sqrt(NB)).reshape(2, L // 2, COLS)
    return table.reshape(16, 2 * PADB)


def make_table(tw_ref, base_ref, table_ref):
    for a in range(16):
        for v in range(PADB // 128):
            c_cols = slice(128 * v, 128 * v + 128)
            s_cols = slice(PADB + 128 * v, PADB + 128 * v + 128)
            fc, fs = tw_ref[0:16, c_cols], tw_ref[0:16, s_cols]
            mc, ms = tw_ref[16 + a : 17 + a, c_cols], tw_ref[16 + a : 17 + a, s_cols]
            base_ref[16 * a : 16 * a + 16, c_cols] = fc * mc - fs * ms
            base_ref[16 * a : 16 * a + 16, s_cols] = fs * mc + fc * ms

    def chunk(i, carry):
        row0 = pl.multiple_of(i * CHUNK, CHUNK)
        for v in range(PADB // 128):
            c_cols = slice(128 * v, 128 * v + 128)
            s_cols = slice(PADB + 128 * v, PADB + 128 * v + 128)
            at = pl.ds(pl.multiple_of(32 + 8 * i, 8), 8)
            cc = jnp.concatenate([tw_ref[at, c_cols]] * 2, axis=0)
            cs = jnp.concatenate([tw_ref[at, s_cols]] * 2, axis=0)
            for r in range(0, CHUNK, 16):
                bc, bs = base_ref[r : r + 16, c_cols], base_ref[r : r + 16, s_cols]
                rows = pl.ds(row0 + r, 16)
                table_ref[rows, c_cols] = (bc * cc - bs * cs).astype(jnp.bfloat16)
                table_ref[rows, s_cols] = (bs * cc + bc * cs).astype(jnp.bfloat16)
        return carry

    lax.fori_loop(0, NCHUNK, chunk, 0)


def whiten_rows(spec_ref, slots):
    def quarter(q, part):
        return spec_ref[slots * q : slots * (q + 1), PADB * part : PADB * (part + 1)]

    a0, a1, a2, a3 = (quarter(q, 0) for q in range(4))
    b0, b1, b2, b3 = (quarter(q, 1) for q in range(4))
    m = lax.broadcasted_iota(jnp.int32, (slots, PADB), 1) % 4
    even = m % 2 == 0
    sign = jnp.where(m < 2, 1.0, -1.0)
    re = jnp.where(even, a0 + a2 + sign * (a1 + a3), a0 - a2 + sign * (b1 - b3))
    im = jnp.where(even, b0 + b2 + sign * (b1 + b3), b0 - b2 - sign * (a1 - a3))
    mag = re * re + im * im
    power = jnp.sum(mag, axis=1, keepdims=True) / NB
    denom = jnp.sqrt(mag + WATER * power + 1e-06)
    re, im = re / denom, im / denom
    tail = re[:, 384:] + pltpu.roll(im[:, 384:], 64, 1)
    return jnp.concatenate([re[:, :384], im[:, :384], tail], axis=1).astype(jnp.bfloat16)


def kernel(
    n,
    raw_hbm,
    index_ref,
    count_ref,
    tw_hbm,
    out_ref,
    tw_ref,
    x_ref,
    xq_ref,
    base_ref,
    table_ref,
    spec_ref,
    spread_ref,
    lagged_ref,
    load_sem,
    tw_sem,
    zsend_sem,
    zrecv_sem,
    xsend_sem,
    xrecv_sem,
    fsend_sem,
    frecv_sem,
):
    slots = raw_hbm.shape[0]
    half = slots // 2
    me = lax.axis_index("chan")
    core = lax.axis_index("pair")
    other = 1 - core

    load = pltpu.make_async_copy(raw_hbm, x_ref, load_sem)
    tw_load = pltpu.make_async_copy(tw_hbm, tw_ref, tw_sem)
    tw_load.start()
    load.start()

    lines = n // 2
    line, side = me // 2, lax.rem(me, 2)
    mate = 2 * line + 1 - side
    order = list(range(1, lines))

    def chip(d, which):
        row = line
        for bit in range(lines.bit_length()):
            if d >> bit & 1:
                row = row + (1 << bit) - (2 << bit) * (line // (1 << bit) % 2)
        return 2 * row + which

    barrier = pltpu.get_barrier_semaphore()
    pl.semaphore_signal(barrier, inc=1, device_id={"pair": other})
    pl.semaphore_signal(barrier, inc=1, device_id={"chan": mate})
    for d in order:
        pl.semaphore_signal(barrier, inc=1, device_id={"chan": chip(d, side)})

    tw_load.wait()
    make_table(tw_ref, base_ref, table_ref)
    load.wait()
    for q in range(4):
        rows = slice(slots * q, slots * (q + 1))
        xq_ref[rows, 0:QUARTER] = x_ref[:, QUARTER * q : QUARTER * (q + 1)]
        pad = NCHUNK * CHUNK - QUARTER
        xq_ref[rows, QUARTER:] = jnp.zeros((slots, pad), jnp.bfloat16)
    for v in range(2 * PADB // 256):
        cols = slice(256 * v, 256 * v + 256)
        spec_ref[:, cols] = jnp.dot(
            xq_ref[...], table_ref[:, cols], preferred_element_type=jnp.float32
        )
    whitened = whiten_rows(spec_ref, slots)

    r_ids = lax.broadcasted_iota(jnp.int32, (slots, slots), 0)
    k_ids = lax.broadcasted_iota(jnp.int32, (slots, slots), 1)
    chosen = (index_ref[...] == r_ids) & (k_ids < count_ref[me])
    pick = jnp.where(chosen, 1.0, 0.0).T.astype(jnp.bfloat16)
    own = jnp.dot(pick, whitened, preferred_element_type=jnp.float32)
    own16 = own.astype(jnp.bfloat16)
    spread_ref[pl.ds(pl.multiple_of(me * slots, slots), slots), :] = own16

    def part(block, who):
        return spread_ref.at[pl.ds(pl.multiple_of(block * slots + who * half, half), half), :]

    pl.semaphore_wait(barrier, lines + 1)

    def copy(block, who, sends, recvs, at, device_id):
        ref = part(block, who)
        return pltpu.make_async_remote_copy(
            src_ref=ref,
            dst_ref=ref,
            send_sem=sends.at[at],
            recv_sem=recvs.at[at],
            device_id=device_id,
        )

    def along(d, block):
        return copy(block, core, zsend_sem, zrecv_sem, d, {"chan": chip(d, side)})

    def across(d, which):
        return copy(chip(d, which), core, xsend_sem, xrecv_sem, d, {"chan": mate})

    def inside(d, which, who):
        at = d + lines * (1 if which is side else 0)
        return copy(chip(d, which), who, fsend_sem, frecv_sem, at, {"pair": other})

    far = 1 - side
    across(0, side).start()
    for d in order:
        along(d, me).start()
    lag_at = pl.multiple_of(32 + 8 * NCHUNK + 8 * core, 8)
    weights = tw_ref[pl.ds(lag_at, 8), :COLS]
    for l in range(L // 2):
        weight = weights[l : l + 1, :]
        lagged_ref[slots * l : slots * (l + 1), :] = (own * weight).astype(jnp.bfloat16)

    across(0, far).wait_recv()
    inside(0, far, core).start()
    for d in order:
        along(d, chip(d, side)).wait_recv()
        across(d, side).start()
        inside(d, side, core).start()

    for i, d in enumerate([0] + order):
        if d > 0:
            across(d, far).wait_recv()
            inside(d, far, core).start()
            inside(d, side, other).wait_recv()
        inside(d, far, other).wait_recv()
        at = pl.multiple_of(chip(d, 0) * slots, 2 * slots)
        product = lax.dot_general(
            lagged_ref[...],
            spread_ref[pl.ds(at, 2 * slots), :],
            (((1,), (1,)), ((), ())),
            preferred_element_type=jnp.float32,
        ).astype(jnp.bfloat16)
        for l in range(L // 2):
            out_ref[l, :, pl.ds(at, 2 * slots)] = product[slots * l : slots * (l + 1)]

    for d in [0] + order:
        across(d, side).wait_send()
        inside(d, far, core).wait_send()
        if d > 0:
            along(d, me).wait_send()
            inside(d, side, core).wait_send()


def shards(n, raw, live_index, live_count):
    slots = raw.shape[0]
    vmem = pl.BlockSpec(memory_space=pltpu.VMEM)
    return pl.pallas_call(
        functools.partial(kernel, n),
        out_shape=pltpu.VMEM((L // 2, slots, n * slots), jnp.bfloat16),
        in_specs=[
            pl.BlockSpec(memory_space=pl.ANY),
            vmem,
            pl.BlockSpec(memory_space=pltpu.SMEM),
            pl.BlockSpec(memory_space=pl.ANY),
        ],
        out_specs=vmem,
        scratch_shapes=[
            pltpu.VMEM((48 + 8 * NCHUNK, 2 * PADB), jnp.float32),
            pltpu.VMEM((slots, S), jnp.bfloat16),
            pltpu.VMEM((4 * slots, NCHUNK * CHUNK), jnp.bfloat16),
            pltpu.VMEM((CHUNK, 2 * PADB), jnp.float32),
            pltpu.VMEM((NCHUNK * CHUNK, 2 * PADB), jnp.bfloat16),
            pltpu.VMEM((4 * slots, 2 * PADB), jnp.float32),
            pltpu.VMEM((n * slots, COLS), jnp.bfloat16),
            pltpu.VMEM((L // 2 * slots, COLS), jnp.bfloat16),
            pltpu.SemaphoreType.DMA,
            pltpu.SemaphoreType.DMA,
            pltpu.SemaphoreType.DMA((n // 2,)),
            pltpu.SemaphoreType.DMA((n // 2,)),
            pltpu.SemaphoreType.DMA((n // 2,)),
            pltpu.SemaphoreType.DMA((n // 2,)),
            pltpu.SemaphoreType.DMA((n,)),
            pltpu.SemaphoreType.DMA((n,)),
        ],
        compiler_params=pltpu.CompilerParams(
            collective_id=0, has_side_effects=True, vmem_limit_bytes=VMEM_LIMIT - 6 * slots * n * slots
        ),
    )(
        raw.reshape(slots, S),
        live_index,
        live_count,
        jnp.asarray(constants()),
    )


def solution(mesh):
    return jax.shard_map(
        functools.partial(shards, mesh.shape["chan"]),
        mesh=mesh,
        in_specs=(P(("groups", "chan"), None, None), P(("groups", "chan"), None), P("groups")),
        out_specs=P("pair", ("groups", "chan"), None),
        check_vma=False,
    )
```

```python
import functools

import jax
import jax.numpy as jnp
import numpy as np
from jax import lax
from jax.experimental import pallas as pl
from jax.experimental.pallas import tpu as pltpu
from jax.sharding import PartitionSpec as P

S = 12000
NB = 448
L = 6
LSTEP = 125
F0 = 60
WATER = 0.1
QUARTER = S // 4
CHUNK = 256
NCHUNK = -(-QUARTER // CHUNK)
PADB = 512
COLS = 2 * NB
VMEM_LIMIT = 63_300_000


def phase_rows(steps, shift=0.0):
    k = F0 + np.arange(NB)
    angle = 2.0 * np.pi * ((np.asarray(steps)[:, None] * k[None, :]) % S) / S + shift
    out = np.zeros((len(steps), 2 * PADB), np.float32)
    out[:, :NB] = np.cos(angle)
    out[:, PADB : PADB + NB] = -np.sin(angle)
    return out


def constants():
    step = 2.0 * np.pi / S
    fine = phase_rows(np.arange(16), np.pi * (float(np.float32(step)) / step - 1.0))
    mid = phase_rows(16 * np.arange(16))
    coarse = np.repeat(phase_rows(CHUNK * np.arange(NCHUNK)), 8, axis=0)
    return np.concatenate([fine, mid, coarse, lag_table()], axis=0)


def column_bins():
    tail = np.arange(384, NB)
    return np.concatenate([np.arange(384), np.arange(384), tail, tail])


def lag_table():
    j = column_bins()
    taper = 0.5 - 0.5 * np.cos(2.0 * np.pi * (j + 0.5) / NB)
    lags = np.arange(L)[:, None] * LSTEP
    waves = np.cos(2.0 * np.pi * (((F0 + j)[None, :] * lags) % S) / S)
    table = np.zeros((2, 8, 2 * PADB), np.float32)
    table[:, : L // 2, :COLS] = (taper[None, :] * waves / np.sqrt(NB)).reshape(2, L // 2, COLS)
    return table.reshape(16, 2 * PADB)


def make_table(tw_ref, base_ref, table_ref):
    for a in range(16):
        for v in range(PADB // 128):
            c_cols = slice(128 * v, 128 * v + 128)
            s_cols = slice(PADB + 128 * v, PADB + 128 * v + 128)
            fc, fs = tw_ref[0:16, c_cols], tw_ref[0:16, s_cols]
            mc, ms = tw_ref[16 + a : 17 + a, c_cols], tw_ref[16 + a : 17 + a, s_cols]
            base_ref[16 * a : 16 * a + 16, c_cols] = fc * mc - fs * ms
            base_ref[16 * a : 16 * a + 16, s_cols] = fs * mc + fc * ms

    def chunk(i, carry):
        row0 = pl.multiple_of(i * CHUNK, CHUNK)
        for v in range(PADB // 128):
            c_cols = slice(128 * v, 128 * v + 128)
            s_cols = slice(PADB + 128 * v, PADB + 128 * v + 128)
            at = pl.ds(pl.multiple_of(32 + 8 * i, 8), 8)
            cc = jnp.concatenate([tw_ref[at, c_cols]] * 2, axis=0)
            cs = jnp.concatenate([tw_ref[at, s_cols]] * 2, axis=0)
            for r in range(0, CHUNK, 16):
                bc, bs = base_ref[r : r + 16, c_cols], base_ref[r : r + 16, s_cols]
                rows = pl.ds(row0 + r, 16)
                table_ref[rows, c_cols] = (bc * cc - bs * cs).astype(jnp.bfloat16)
                table_ref[rows, s_cols] = (bs * cc + bc * cs).astype(jnp.bfloat16)
        return carry

    lax.fori_loop(0, NCHUNK, chunk, 0)


def whiten_rows(spec_ref, slots):
    def quarter(q, part):
        return spec_ref[slots * q : slots * (q + 1), PADB * part : PADB * (part + 1)]

    a0, a1, a2, a3 = (quarter(q, 0) for q in range(4))
    b0, b1, b2, b3 = (quarter(q, 1) for q in range(4))
    m = lax.broadcasted_iota(jnp.int32, (slots, PADB), 1) % 4
    even = m % 2 == 0
    sign = jnp.where(m < 2, 1.0, -1.0)
    re = jnp.where(even, a0 + a2 + sign * (a1 + a3), a0 - a2 + sign * (b1 - b3))
    im = jnp.where(even, b0 + b2 + sign * (b1 + b3), b0 - b2 - sign * (a1 - a3))
    mag = re * re + im * im
    power = jnp.sum(mag, axis=1, keepdims=True) / NB
    denom = jnp.sqrt(mag + WATER * power + 1e-06)
    re, im = re / denom, im / denom
    tail = re[:, 384:] + pltpu.roll(im[:, 384:], 64, 1)
    return jnp.concatenate([re[:, :384], im[:, :384], tail], axis=1).astype(jnp.bfloat16)


def kernel(
    n,
    raw_hbm,
    index_ref,
    count_ref,
    tw_hbm,
    out_ref,
    tw_ref,
    x_ref,
    xq_ref,
    base_ref,
    table_ref,
    spec_ref,
    spread_ref,
    lagged_ref,
    load_sem,
    tw_sem,
    zsend_sem,
    zrecv_sem,
    xsend_sem,
    xrecv_sem,
    fsend_sem,
    frecv_sem,
):
    slots = raw_hbm.shape[0]
    half = slots // 2
    me = lax.axis_index("chan")
    core = lax.axis_index("pair")
    other = 1 - core

    load = pltpu.make_async_copy(raw_hbm, x_ref, load_sem)
    tw_load = pltpu.make_async_copy(tw_hbm, tw_ref, tw_sem)
    tw_load.start()
    load.start()

    lines = n // 2
    line, side = me // 2, lax.rem(me, 2)
    mate = 2 * line + 1 - side
    order = list(range(1, lines))

    def chip(d, which):
        row = line
        for bit in range(lines.bit_length()):
            if d >> bit & 1:
                row = row + (1 << bit) - (2 << bit) * (line // (1 << bit) % 2)
        return 2 * row + which

    barrier = pltpu.get_barrier_semaphore()
    pl.semaphore_signal(barrier, inc=1, device_id={"pair": other})
    pl.semaphore_signal(barrier, inc=1, device_id={"chan": mate})
    for d in order:
        pl.semaphore_signal(barrier, inc=1, device_id={"chan": chip(d, side)})

    tw_load.wait()
    make_table(tw_ref, base_ref, table_ref)
    load.wait()
    for q in range(4):
        rows = slice(slots * q, slots * (q + 1))
        xq_ref[rows, 0:QUARTER] = x_ref[:, QUARTER * q : QUARTER * (q + 1)]
        pad = NCHUNK * CHUNK - QUARTER
        xq_ref[rows, QUARTER:] = jnp.zeros((slots, pad), jnp.bfloat16)
    for v in range(2 * PADB // 256):
        cols = slice(256 * v, 256 * v + 256)
        spec_ref[:, cols] = jnp.dot(
            xq_ref[...], table_ref[:, cols], preferred_element_type=jnp.float32
        )
    whitened = whiten_rows(spec_ref, slots)

    r_ids = lax.broadcasted_iota(jnp.int32, (slots, slots), 0)
    k_ids = lax.broadcasted_iota(jnp.int32, (slots, slots), 1)
    chosen = (index_ref[...] == r_ids) & (k_ids < count_ref[me])
    pick = jnp.where(chosen, 1.0, 0.0).T.astype(jnp.bfloat16)
    own = jnp.dot(pick, whitened, preferred_element_type=jnp.float32)
    own16 = own.astype(jnp.bfloat16)
    spread_ref[pl.ds(pl.multiple_of(me * slots, slots), slots), :] = own16

    def part(block, who):
        return spread_ref.at[pl.ds(pl.multiple_of(block * slots + who * half, half), half), :]

    pl.semaphore_wait(barrier, lines + 1)

    def copy(block, who, sends, recvs, at, device_id):
        ref = part(block, who)
        return pltpu.make_async_remote_copy(
            src_ref=ref,
            dst_ref=ref,
            send_sem=sends.at[at],
            recv_sem=recvs.at[at],
            device_id=device_id,
        )

    def along(d, block):
        return copy(block, core, zsend_sem, zrecv_sem, d, {"chan": chip(d, side)})

    def across(d, which):
        return copy(chip(d, which), core, xsend_sem, xrecv_sem, d, {"chan": mate})

    def inside(d, which, who):
        at = d + lines * (1 if which is side else 0)
        return copy(chip(d, which), who, fsend_sem, frecv_sem, at, {"pair": other})

    far = 1 - side
    across(0, side).start()
    for d in reversed(order):
        along(d, me).start()
    lag_at = pl.multiple_of(32 + 8 * NCHUNK + 8 * core, 8)
    weights = tw_ref[pl.ds(lag_at, 8), :COLS]
    for l in range(L // 2):
        weight = weights[l : l + 1, :]
        lagged_ref[slots * l : slots * (l + 1), :] = (own * weight).astype(jnp.bfloat16)

    across(0, far).wait_recv()
    inside(0, far, core).start()
    for d in order:
        along(d, chip(d, side)).wait_recv()
        across(d, side).start()
        inside(d, side, core).start()

    for i, d in enumerate([0] + order):
        if d > 0:
            across(d, far).wait_recv()
            inside(d, far, core).start()
            inside(d, side, other).wait_recv()
        inside(d, far, other).wait_recv()
        at = pl.multiple_of(chip(d, 0) * slots, 2 * slots)
        product = lax.dot_general(
            lagged_ref[...],
            spread_ref[pl.ds(at, 2 * slots), :],
            (((1,), (1,)), ((), ())),
            preferred_element_type=jnp.float32,
        ).astype(jnp.bfloat16)
        for l in range(L // 2):
            out_ref[l, :, pl.ds(at, 2 * slots)] = product[slots * l : slots * (l + 1)]

    for d in [0] + order:
        across(d, side).wait_send()
        inside(d, far, core).wait_send()
        if d > 0:
            along(d, me).wait_send()
            inside(d, side, core).wait_send()


def shards(n, raw, live_index, live_count):
    slots = raw.shape[0]
    vmem = pl.BlockSpec(memory_space=pltpu.VMEM)
    return pl.pallas_call(
        functools.partial(kernel, n),
        out_shape=pltpu.VMEM((L // 2, slots, n * slots), jnp.bfloat16),
        in_specs=[
            pl.BlockSpec(memory_space=pl.ANY),
            vmem,
            pl.BlockSpec(memory_space=pltpu.SMEM),
            pl.BlockSpec(memory_space=pl.ANY),
        ],
        out_specs=vmem,
        scratch_shapes=[
            pltpu.VMEM((48 + 8 * NCHUNK, 2 * PADB), jnp.float32),
            pltpu.VMEM((slots, S), jnp.bfloat16),
            pltpu.VMEM((4 * slots, NCHUNK * CHUNK), jnp.bfloat16),
            pltpu.VMEM((CHUNK, 2 * PADB), jnp.float32),
            pltpu.VMEM((NCHUNK * CHUNK, 2 * PADB), jnp.bfloat16),
            pltpu.VMEM((4 * slots, 2 * PADB), jnp.float32),
            pltpu.VMEM((n * slots, COLS), jnp.bfloat16),
            pltpu.VMEM((L // 2 * slots, COLS), jnp.bfloat16),
            pltpu.SemaphoreType.DMA,
            pltpu.SemaphoreType.DMA,
            pltpu.SemaphoreType.DMA((n // 2,)),
            pltpu.SemaphoreType.DMA((n // 2,)),
            pltpu.SemaphoreType.DMA((n // 2,)),
            pltpu.SemaphoreType.DMA((n // 2,)),
            pltpu.SemaphoreType.DMA((n,)),
            pltpu.SemaphoreType.DMA((n,)),
        ],
        compiler_params=pltpu.CompilerParams(
            collective_id=0, has_side_effects=True, vmem_limit_bytes=VMEM_LIMIT - 6 * slots * n * slots
        ),
    )(
        raw.reshape(slots, S),
        live_index,
        live_count,
        jnp.asarray(constants()),
    )


def solution(mesh):
    return jax.shard_map(
        functools.partial(shards, mesh.shape["chan"]),
        mesh=mesh,
        in_specs=(P(("groups", "chan"), None, None), P(("groups", "chan"), None), P("groups")),
        out_specs=P("pair", ("groups", "chan"), None),
        check_vma=False,
    )
```
